512 devices in a mesh: visit: 8 (over z), strip: 64 (over y, x, core).
Axes of the slice: x: 4, y: 8, z: 8, core: 2. Of those that a mesh axis runs over, the one named last changes fastest.
Arguments:
- template: bfloat16 [2048, 1024], P('strip', 'visit'), may hold values from -60 to 60
- science_src: bfloat16 [8, 4096, 1024], P('visit', 'strip'), may hold values from -180 to 180
- target_rows: int32 [8, 4096], P('visit'), may hold values from 0 to 2047, as said below
- row_taps: bfloat16 [45, 21], replicated, may hold values from -1.25 to 1.25
- col_taps: bfloat16 [45, 21], replicated, may hold values from -1.25 to 1.25
Outputs:
- difference: float32 [8, 2048, 1024], P('visit', 'strip')
- kernel_coeffs: float32 [8, 45], P('visit')
The draws below stay inside these ranges and needn't reach their ends.
Inputs may be any that keep to these rules, and one draw needn't show every extreme that they name: `target_rows`: row j of a visit lies on strip device j // 64; its target's strip is target // 32. Of the 64 rows of one strip device at most 2 target the same strip, and in every visit one strip receives exactly 2 rows from every strip device.
All inputs are finite; a program needn't handle non-finite values.
Results may differ from the reference program's by a relative error of at most 0.0014.
Values may be sent and summed in bfloat16 or wider, within the bound.
No kernel may reach another device: no remote copies, remote signals or barrier semaphores. Data moves between devices by JAX's collectives and lax.ppermute only.
A program may use at most 64 MiB of HBM per device.

```python
import math
import jax
import jax.numpy as jnp
from jax import lax

NBASIS = 45
TAPS = 21
ROWS_DEV = 32
COLS = 1024
SRC_DEV = 64
CAP = 2
VISITS = 8
NROWS = 2048


def strip_routes(key):
    route_key = jax.random.fold_in(key, 11)
    sub_keys = jax.random.split(route_key, 4)
    strips = NROWS // ROWS_DEV
    others = (strips - 1) * CAP
    busiest = jax.random.randint(sub_keys[0], (VISITS, 1, 1), 0, strips)
    pick_keys = jax.random.split(sub_keys[1], VISITS * strips)
    chosen = jax.vmap(lambda k: jax.random.permutation(k, others)[:SRC_DEV - CAP])(pick_keys)
    chosen = chosen.reshape(VISITS, strips, SRC_DEV - CAP)
    spread_dest = chosen // CAP
    spread_dest = spread_dest + (spread_dest >= busiest).astype(jnp.int32)
    full_dest = jnp.broadcast_to(busiest, (VISITS, strips, CAP))
    listed = jnp.concatenate([full_dest, spread_dest], axis=2)
    mix_keys = jax.random.split(sub_keys[2], VISITS * strips)
    mixing = jax.vmap(lambda k: jax.random.permutation(k, SRC_DEV))(mix_keys).reshape(VISITS, strips, SRC_DEV)
    dest_strip = jnp.take_along_axis(listed, mixing, axis=2)
    row_pick = jax.random.randint(sub_keys[3], (VISITS, strips, SRC_DEV), 0, ROWS_DEV)
    return (dest_strip * ROWS_DEV + row_pick).reshape(VISITS, strips * SRC_DEV).astype(jnp.int32)


def template_field(key):
    sub_keys = jax.random.split(jax.random.fold_in(key, 23), 3)
    row_pos = jnp.arange(NROWS, dtype=jnp.float32) / NROWS
    trend = 0.6 + 0.8 * row_pos
    values = jnp.clip(jax.random.normal(sub_keys[0], (NROWS, COLS), jnp.float32), -4.0, 4.0)
    row_scale = jnp.exp(math.log(10.0) * (jax.random.uniform(sub_keys[1], (NROWS,), jnp.float32) - 0.5))
    col_scale = jnp.exp(math.log(10.0) * (jax.random.uniform(sub_keys[2], (COLS,), jnp.float32) - 0.5))
    return values * (trend * row_scale)[:, None] * col_scale[None, :]


def draw_template(key, part):
    return template_field(key).astype(jnp.bfloat16)


def draw_target_rows(key, part):
    return strip_routes(key)


def draw_science_src(key, part):
    field = template_field(key)
    targets = strip_routes(key)
    sub_keys = jax.random.split(jax.random.fold_in(key, 31), 2)
    visit_gain = jnp.exp(math.log(2.0) * jax.random.uniform(sub_keys[0], (VISITS, 1), jnp.float32, -1.0, 1.0))
    gain = (0.5 + targets.astype(jnp.float32) / NROWS) * visit_gain
    picked = field[targets]
    noise = 0.5 * jnp.clip(jax.random.normal(sub_keys[1], picked.shape, jnp.float32), -4.0, 4.0)
    return (gain[..., None] * picked + noise).astype(jnp.bfloat16)


def bell_draw(own_key, dims, deviation, most, kind=jnp.bfloat16):
    return jnp.clip(deviation * jax.random.normal(own_key, dims, jnp.float32), -most, most).astype(kind)


def setup_inputs(seed: int = 0) -> dict:
    key_of = jax.random.split(jax.random.key(seed), 6)
    template = draw_template(jax.random.fold_in(key_of[5], 71), 0)
    science_src = draw_science_src(jax.random.fold_in(key_of[5], 71), 0)
    target_rows = draw_target_rows(jax.random.fold_in(key_of[5], 71), 0)
    row_taps = bell_draw(key_of[3], (NBASIS, TAPS), TAPS ** -0.5, 1.25)
    col_taps = bell_draw(key_of[4], (NBASIS, TAPS), TAPS ** -0.5, 1.25)
    return dict(template=template, science_src=science_src, target_rows=target_rows, row_taps=row_taps, col_taps=col_taps)


PRECISE = lax.Precision.HIGHEST

def strip_basis(window, row_taps, col_taps):
    tap_count = col_taps.shape[1]
    out_width = window.shape[1] - tap_count + 1
    out_rows = window.shape[0] - tap_count + 1
    shifted = jnp.stack([window[:, t:t + out_width] for t in range(tap_count)]).astype(jnp.float32)
    smoothed = jnp.einsum('kt,thw->khw', col_taps.astype(jnp.float32), shifted, precision=PRECISE)
    smoothed = lax.optimization_barrier(smoothed.astype(jnp.bfloat16)).astype(jnp.float32)
    summed = jnp.zeros((row_taps.shape[0], out_rows, out_width), jnp.float32)
    for s in range(tap_count):
        summed = summed + row_taps[:, s].astype(jnp.float32)[:, None, None] * smoothed[:, s:s + out_rows, :]
    return summed.astype(jnp.bfloat16)

def solve_normal(gram_total, moment):
    factor = jnp.linalg.cholesky(gram_total)
    forward = lax.linalg.triangular_solve(factor, moment.T, left_side=True, lower=True)
    answer = lax.linalg.triangular_solve(factor, forward, left_side=True, lower=True, transpose_a=True)
    return answer.T

def reference(template, science_src, target_rows, row_taps, col_taps):
    margin = (row_taps.shape[1] - 1) // 2
    basis_count = row_taps.shape[0]
    science = jax.vmap(lambda source_rows, row_targets: jax.ops.segment_sum(source_rows.astype(jnp.float32), row_targets, num_segments=NROWS))(science_src, target_rows)
    framed = jnp.pad(template, ((margin, margin), (margin, margin)))
    strips = NROWS // ROWS_DEV

    def strip_images(index):
        window = lax.dynamic_slice_in_dim(framed, index * ROWS_DEV, ROWS_DEV + 2 * margin, 0)
        return strip_basis(window, row_taps, col_taps).astype(jnp.float32).reshape(basis_count, ROWS_DEV * COLS)

    def strip_science(index):
        return lax.dynamic_slice_in_dim(science, index * ROWS_DEV, ROWS_DEV, 1).reshape(VISITS, ROWS_DEV * COLS)

    def accumulate(running, index):
        gram_total, moment = running
        images = strip_images(index)
        gram_total = gram_total + jnp.dot(images, images.T, precision=PRECISE)
        moment = moment + jnp.einsum('kp,vp->vk', images, strip_science(index), precision=PRECISE)
        return ((gram_total, moment), None)
    start = (jnp.zeros((basis_count, basis_count), jnp.float32), jnp.zeros((VISITS, basis_count), jnp.float32))
    (gram_total, moment), _ = lax.scan(accumulate, start, jnp.arange(strips, dtype=jnp.int32))
    kernel_coeffs = solve_normal(gram_total, moment)

    def difference_rows(index):
        images = strip_images(index)
        model = jnp.einsum('vk,kp->vp', kernel_coeffs, images, precision=PRECISE)
        return (strip_science(index) - model).reshape(VISITS, ROWS_DEV, COLS)
    pieces = lax.map(difference_rows, jnp.arange(strips, dtype=jnp.int32))
    difference = jnp.transpose(pieces, (1, 0, 2, 3)).reshape(VISITS, NROWS, COLS)
    return (difference, kernel_coeffs)
```

```python
import jax
import jax.numpy as jnp
from jax import lax
from jax.experimental import pallas as pl
from jax.experimental.pallas import tpu as pltpu
from jax.sharding import Mesh, PartitionSpec as P

STRIPS = 64
VISITS = 8
ROWS = 32
COLS = 1024
LANES = 128
SRC = 64
TAPS = 21
REACH = 10
NB = 45
PAD = 48
HALO = 16
FRAME = ROWS + 2 * HALO
QUAD = 4
SUB = 8
BIG = 1 << 20
F32 = jnp.float32
BF16 = jnp.bfloat16
STRIP = ("y", "x", "core")


def vmem(count):
    return [pl.BlockSpec(memory_space=pltpu.VMEM)] * count


def iota(shape, dim):
    return lax.broadcasted_iota(jnp.int32, shape, dim)


def send_kernel(mine_ref, src_ref, out_ref):
    dest = mine_ref[...] // ROWS
    at_dest = dest == iota((STRIPS, SRC), 0)
    order = iota((STRIPS, SRC), 1)
    first = jnp.min(jnp.where(at_dest, order, BIG), axis=1, keepdims=True)
    last = jnp.max(jnp.where(at_dest, order, -1), axis=1, keepdims=True)
    src = src_ref[...]
    one = at_dest & (order == first)
    two = at_dest & (order == last) & (last != first)
    for slot, pick in enumerate((one, two)):
        rows = jnp.dot(pick.astype(F32).astype(BF16), src, preferred_element_type=F32)
        out_ref[:, slot * COLS:(slot + 1) * COLS] = rows.astype(BF16)


def basis_kernel(tile_ref, row_ref, col_ref, basis_ref, gram_ref, win_ref, wide_ref):
    zero = jnp.zeros((FRAME, LANES // 2), BF16)
    blocks = [tile_ref[b] for b in range(VISITS)]
    halves = [zero]
    for b in range(VISITS):
        halves += [blocks[b][:, :LANES // 2], blocks[b][:, LANES // 2:]]
    halves.append(zero)
    shifted = [jnp.concatenate([halves[2 * i], halves[2 * i + 1]], axis=1) for i in range(VISITS + 1)]
    for b in range(VISITS):
        win_ref[b * FRAME:(b + 1) * FRAME, :LANES] = shifted[b]
        win_ref[b * FRAME:(b + 1) * FRAME, LANES:] = shifted[b + 1]
    above = iota((LANES, LANES), 1) <= iota((LANES, LANES), 0) - (LANES // 2 - REACH)

    def quad(q, carry):
        smooth = []
        bands = []
        for pair in range(QUAD // 2):
            tops, bottoms = [], []
            for j in range(2):
                k = q * QUAD + pair * 2 + j
                taps = jnp.broadcast_to(col_ref[pl.ds(k, 1), :], (LANES, LANES))
                wheel = pltpu.roll(taps, 0, 1, stride=1, stride_axis=0)
                tops.append(jnp.where(above, wheel, 0.0).astype(BF16))
                bottoms.append(jnp.where(above, 0.0, wheel).astype(BF16))
            band = jnp.concatenate(
                [jnp.concatenate(tops, axis=1), jnp.concatenate(bottoms, axis=1)], axis=0
            )
            both = jnp.dot(win_ref[...], band, preferred_element_type=F32).astype(BF16)
            smooth += [both[:, :LANES], both[:, LANES:]]
        for j in range(QUAD):
            k = q * QUAD + j
            taps = jnp.broadcast_to(row_ref[pl.ds(k, 1), :], (ROWS, LANES))
            band = pltpu.roll(taps, (j % 2) * FRAME, 1, stride=1, stride_axis=0).astype(BF16)
            blank = jnp.zeros((ROWS, LANES), BF16)
            bands.append(jnp.concatenate([band, blank] if j < 2 else [blank, band], axis=1))
        row_band = jnp.concatenate(bands, axis=0)
        for b in range(0, VISITS, 2):
            stack = jnp.concatenate(
                [
                    jnp.concatenate(
                        [s[b * FRAME:(b + 1) * FRAME], s[(b + 1) * FRAME:(b + 2) * FRAME]], axis=1
                    )
                    for s in smooth
                ],
                axis=0,
            )
            done = jnp.dot(row_band, stack, preferred_element_type=F32)
            for j in range(QUAD):
                for half in range(2):
                    wide_ref[b + half, pl.ds(q * QUAD + j, ROWS, stride=PAD), :] = done[
                        j * ROWS:(j + 1) * ROWS, half * LANES:(half + 1) * LANES
                    ]
        return carry

    lax.fori_loop(0, PAD // QUAD, quad, 0)

    def gram_step(r, total):
        at = pl.multiple_of(r * PAD, PAD)
        images = jnp.concatenate(
            [wide_ref[b, pl.ds(at, PAD), :].astype(BF16) for b in range(VISITS)], axis=1
        )
        basis_ref[pl.ds(at, PAD), :] = images
        return total + lax.dot_general(
            images, images, (((1,), (1,)), ((), ())), preferred_element_type=F32
        )

    gram_ref[...] = lax.fori_loop(0, ROWS, gram_step, jnp.zeros((PAD, PAD), F32))


def moment_kernel(me_ref, targets_ref, got_ref, basis_ref, gram_ref, science_ref, part_ref):
    targets = targets_ref[...]
    here = targets // ROWS == me_ref[0]
    key = iota((STRIPS, SRC), 1) * ROWS + targets % ROWS
    first = jnp.min(jnp.where(here, key, BIG), axis=1, keepdims=True)
    last = jnp.max(jnp.where(here, key, -1), axis=1, keepdims=True)
    rows = iota((STRIPS, ROWS), 1)
    one = (first < BIG) & (first % ROWS == rows)
    two = (last >= 0) & (last != first) & (last % ROWS == rows)
    science = jnp.zeros((ROWS, COLS), F32)
    for slot, hit in enumerate((one, two)):
        science = science + lax.dot_general(
            hit.astype(F32).astype(BF16),
            got_ref[:, slot * COLS:(slot + 1) * COLS],
            (((0,), (0,)), ((), ())),
            preferred_element_type=F32,
        )
    science_ref[...] = science

    def step(g, total):
        for b in range(VISITS):
            cut = slice(b * LANES, (b + 1) * LANES)
            lines = science_ref[pl.ds(pl.multiple_of(g * SUB, SUB), SUB), cut]
            for i in range(SUB):
                at = pl.multiple_of((g * SUB + i) * PAD, PAD)
                images = basis_ref[pl.ds(at, PAD), cut].astype(F32)
                total = total + images * lines[i:i + 1, :]
        return total

    total = lax.fori_loop(0, ROWS // SUB, step, jnp.zeros((PAD, LANES), F32))
    moment = jnp.sum(total, axis=1, keepdims=True)
    lane = iota((PAD, LANES), 1)
    gram = jnp.concatenate([gram_ref[...], jnp.zeros((PAD, LANES - PAD), F32)], axis=1)
    part_ref[...] = jnp.where(lane == NB, moment, gram)


def solve_kernel(parts_ref, basis_ref, science_ref, diff_ref, coeff_ref):
    system = parts_ref[0]
    for i in range(1, parts_ref.shape[0]):
        system = system + parts_ref[i]
    sub = iota((PAD, LANES), 0)
    lane = iota((PAD, LANES), 1)
    for p in range(NB):
        column = jnp.broadcast_to(system[:, p:p + 1], (PAD, LANES))
        row = system[p:p + 1, :] / column[p:p + 1, :]
        system = jnp.where(sub == p, row, system - column * row)
    answer = jnp.broadcast_to(system[:, NB:NB + 1], (PAD, LANES))
    coeff_ref[...] = jnp.sum(jnp.where(sub == lane, answer, 0.0), axis=0, keepdims=True)

    def step(g, carry):
        for b in range(VISITS):
            cut = slice(b * LANES, (b + 1) * LANES)
            lines = []
            for i in range(SUB):
                at = pl.multiple_of((g * SUB + i) * PAD, PAD)
                images = basis_ref[pl.ds(at, PAD), cut].astype(F32)
                lines.append(jnp.sum(images * answer, axis=0, keepdims=True))
            here = pl.ds(pl.multiple_of(g * SUB, SUB), SUB)
            diff_ref[here, cut] = science_ref[here, cut] - jnp.concatenate(lines, axis=0)
        return carry

    lax.fori_loop(0, ROWS // SUB, step, 0)


def share(block, axis):
    count = lax.axis_size(axis)
    return lax.all_to_all(
        jnp.broadcast_to(block[None], (count,) + block.shape), axis, 0, 0, tiled=True
    )


def body(template, science_src, target_rows, row_taps, col_taps):
    strip = lax.axis_index(STRIP)
    below = [(i, i + 1) for i in range(STRIPS - 1)]
    above = [(i + 1, i) for i in range(STRIPS - 1)]
    head = lax.ppermute(template[ROWS - HALO:], STRIP, below)
    tail = lax.ppermute(template[:HALO], STRIP, above)

    targets = target_rows.reshape(STRIPS, SRC)
    mine = lax.dynamic_slice_in_dim(targets, strip, 1, 0)
    outgoing = pl.pallas_call(
        send_kernel,
        out_shape=jax.ShapeDtypeStruct((STRIPS, 2 * COLS), BF16),
        in_specs=vmem(2),
        out_specs=vmem(1)[0],
        name="send",
    )(mine, science_src[0])
    incoming = lax.all_to_all(
        outgoing.reshape(STRIPS, 2, COLS), STRIP, 0, 0, tiled=True
    ).reshape(STRIPS, 2 * COLS)

    row_lanes = jnp.pad(row_taps.astype(F32), ((0, PAD - NB), (HALO - REACH, LANES - TAPS - HALO + REACH)))
    left = LANES // 2 - REACH
    col_lanes = jnp.pad(
        col_taps[:, ::-1].astype(F32), ((0, PAD - NB), (left, LANES - TAPS - left))
    )

    framed = jnp.concatenate([head, template, tail], axis=0)
    tiles = share(framed, "visit")
    basis, gram = pl.pallas_call(
        basis_kernel,
        out_shape=(
            jax.ShapeDtypeStruct((ROWS * PAD, COLS), BF16),
            jax.ShapeDtypeStruct((PAD, PAD), F32),
        ),
        in_specs=vmem(3),
        out_specs=tuple(vmem(2)),
        scratch_shapes=[
            pltpu.VMEM((VISITS * FRAME, 2 * LANES), BF16),
            pltpu.VMEM((VISITS, ROWS * PAD, LANES), F32),
        ],
        name="basis",
    )(tiles, row_lanes, col_lanes)
    science, part = pl.pallas_call(
        moment_kernel,
        out_shape=(
            jax.ShapeDtypeStruct((ROWS, COLS), F32),
            jax.ShapeDtypeStruct((PAD, LANES), F32),
        ),
        in_specs=[pl.BlockSpec(memory_space=pltpu.SMEM)] + vmem(4),
        out_specs=tuple(vmem(2)),
        name="moment",
    )(strip.reshape(1), targets, incoming, basis, gram)
    near = jnp.sum(share(part, ("x", "core")), axis=0)
    parts = share(near, "y")
    difference, coeffs = pl.pallas_call(
        solve_kernel,
        out_shape=(
            jax.ShapeDtypeStruct((ROWS, COLS), F32),
            jax.ShapeDtypeStruct((1, LANES), F32),
        ),
        in_specs=vmem(3),
        out_specs=tuple(vmem(2)),
        name="solve",
    )(parts, basis, science)
    return difference[None], coeffs[:, :NB]


def solution(mesh):
    sizes = (VISITS, 8, 4, 2)
    fine = Mesh(mesh.devices.reshape(sizes), ("visit",) + STRIP)
    in_specs = (P(STRIP, "visit"), P("visit", STRIP, None), P("visit", None), P(), P())
    out_specs = (P("visit", STRIP, None), P("visit", None))
    return jax.shard_map(body, mesh=fine, in_specs=in_specs, out_specs=out_specs, check_vma=False)
```

```python
import jax
import jax.numpy as jnp
from jax import lax
from jax.experimental import pallas as pl
from jax.experimental.pallas import tpu as pltpu
from jax.sharding import Mesh, PartitionSpec as P

STRIPS = 64
VISITS = 8
ROWS = 32
COLS = 1024
LANES = 128
SRC = 64
TAPS = 21
REACH = 10
NB = 45
PAD = 48
HALO = 16
FRAME = ROWS + 2 * HALO
QUAD = 4
QUADS = PAD // QUAD
SUB = 8
TILE = 16
AHEAD = 3
BIG = 1 << 20
F32 = jnp.float32
BF16 = jnp.bfloat16
STRIP = ("y", "x", "core")
MIB = 1 << 20


def vmem(count):
    return [pl.BlockSpec(memory_space=pltpu.VMEM)] * count


def iota(shape, dim):
    return lax.broadcasted_iota(jnp.int32, shape, dim)


def call(kernel, outs, *args, scratch=(), grant=8, far=0):
    return pl.pallas_call(
        kernel,
        out_shape=tuple(jax.ShapeDtypeStruct(*o) for o in outs),
        in_specs=[pl.BlockSpec(memory_space=pltpu.HBM)] * far + vmem(len(args) - far),
        out_specs=tuple(vmem(len(outs))),
        scratch_shapes=list(scratch),
        compiler_params=pltpu.CompilerParams(vmem_limit_bytes=grant * MIB),
    )(*[pltpu.with_memory_space_constraint(arg, pltpu.HBM) for arg in args[:far]], *args[far:])


def my_strip():
    return (lax.axis_index("y") * 4 + lax.axis_index("x")) * 2 + lax.axis_index("core")


def fetch(pairs, sems):
    copies = [pltpu.make_async_copy(far, near, sems.at[i]) for i, (far, near) in enumerate(pairs)]
    for copy in copies:
        copy.start()
    return copies


def prepare_kernel(targets_hbm, src_hbm, out_ref, targets_ref, src_ref, sems):
    copies = fetch([(targets_hbm, targets_ref), (src_hbm, src_ref)], sems)
    for copy in copies:
        copy.wait()
    send(targets_ref, src_ref, out_ref)


def send(targets_ref, src_ref, out_ref):
    strip = my_strip()
    line = jnp.broadcast_to(targets_ref[pl.ds(strip // 2, 1), :], (SUB, LANES))
    line = pltpu.roll(line, (strip % 2) * SRC, 1)
    dest = line[:1, :SRC] // ROWS
    at_dest = dest == iota((STRIPS, SRC), 0)
    order = iota((STRIPS, SRC), 1)
    first = jnp.min(jnp.where(at_dest, order, BIG), axis=1, keepdims=True)
    last = jnp.max(jnp.where(at_dest, order, -1), axis=1, keepdims=True)
    src = src_ref[...]
    one = at_dest & (order == first)
    two = at_dest & (order == last) & (last != first)
    slots = []
    for pick in (one, two):
        rows = jnp.dot(pick.astype(F32).astype(BF16), src, preferred_element_type=F32)
        slots.append(rows.reshape(STRIPS, SUB, LANES))
    out_ref[...] = jnp.concatenate(slots, axis=1).astype(BF16)


def hits(targets_ref, hit_ref):
    strip = my_strip()
    targets = targets_ref[...]
    key = jnp.where(targets // ROWS == strip, (iota(targets.shape, 1) % SRC) * ROWS + targets % ROWS, BIG)
    swapped = jnp.where(key == BIG, -1, key)
    upper = iota(targets.shape, 1) >= SRC
    rows = iota((STRIPS // 2, ROWS), 1)
    for half in range(2):
        mine = upper if half else ~upper
        first = jnp.min(jnp.where(mine, key, BIG), axis=1, keepdims=True)
        last = jnp.max(jnp.where(mine, swapped, -1), axis=1, keepdims=True)
        one = (first < BIG) & (first % ROWS == rows)
        two = (last >= 0) & (last != first) & (last % ROWS == rows)
        hit_ref[half] = one.astype(F32).astype(BF16)
        hit_ref[2 + half] = two.astype(F32).astype(BF16)


def bands(row_ref, col_ref, row_band_ref, col_band_ref, spread_ref):
    spread_ref[...] = jnp.zeros((LANES, LANES), F32)
    spread_ref[HALO - REACH:HALO - REACH + TAPS, :NB] = row_ref[...].astype(F32)
    row_lines = spread_ref[...].T
    spread_ref[...] = jnp.zeros((LANES, LANES), F32)
    top = LANES // 2 + REACH
    col = col_ref[...].astype(F32)
    for t in range(TAPS):
        spread_ref[top - t:top - t + 1, :NB] = col[t:t + 1]
    col_lines = spread_ref[...].T
    above = iota((LANES, LANES), 1) <= iota((LANES, LANES), 0) - (LANES // 2 - REACH)
    blank = jnp.zeros((ROWS, LANES), BF16)
    for k in range(PAD):
        taps = jnp.broadcast_to(col_lines[k:k + 1], (LANES, LANES))
        wheel = pltpu.roll(taps, 0, 1, stride=1, stride_axis=0)
        cut = slice((k % 2) * LANES, (k % 2 + 1) * LANES)
        col_band_ref[k // 2, :LANES, cut] = jnp.where(above, wheel, 0.0).astype(BF16)
        col_band_ref[k // 2, LANES:, cut] = jnp.where(above, 0.0, wheel).astype(BF16)
        taps = jnp.broadcast_to(row_lines[k:k + 1], (ROWS, LANES))
        j = k % QUAD
        band = pltpu.roll(taps, (j % 2) * FRAME, 1, stride=1, stride_axis=0).astype(BF16)
        here = slice(j * ROWS, (j + 1) * ROWS)
        row_band_ref[k // QUAD, here, :LANES] = band if j < 2 else blank
        row_band_ref[k // QUAD, here, LANES:] = blank if j < 2 else band


def basis_kernel(
    row_hbm, col_hbm, own_hbm, above_ref, below_ref,
    basis_ref, gram_ref,
    row_ref, col_ref, own_ref,
    spread_ref, row_band_ref, col_band_ref, win_ref, even_ref, odd_ref, wide_ref, sems,
):
    copies = fetch([(row_hbm, row_ref), (col_hbm, col_ref), (own_hbm, own_ref)], sems)
    copies[0].wait()
    copies[1].wait()
    bands(row_ref, col_ref, row_band_ref, col_band_ref, spread_ref)
    copies[2].wait()
    zero = jnp.zeros((FRAME, LANES // 2), BF16)
    halves = [zero]
    for b in range(VISITS):
        block = jnp.concatenate(
            [above_ref[b, ROWS - HALO:, :], own_ref[b], below_ref[b, :HALO, :]], axis=0
        )
        halves += [block[:, :LANES // 2], block[:, LANES // 2:]]
    halves.append(zero)
    shifted = [jnp.concatenate([halves[2 * i], halves[2 * i + 1]], axis=1) for i in range(VISITS + 1)]
    for b in range(VISITS):
        win_ref[b * FRAME:(b + 1) * FRAME, :LANES] = shifted[b]
        win_ref[b * FRAME:(b + 1) * FRAME, LANES:] = shifted[b + 1]

    def columns(q, smooth_ref):
        for pair in range(QUAD // 2):
            both = jnp.dot(
                win_ref[...], col_band_ref[q * (QUAD // 2) + pair], preferred_element_type=F32
            ).astype(BF16)
            for half in range(2):
                at = (pair * 2 + half) * FRAME
                for b in range(VISITS):
                    smooth_ref[at:at + FRAME, b * LANES:(b + 1) * LANES] = both[
                        b * FRAME:(b + 1) * FRAME, half * LANES:(half + 1) * LANES
                    ]

    def rows(q, smooth_ref):
        done = jnp.dot(row_band_ref[q], smooth_ref[...], preferred_element_type=F32)
        for j in range(QUAD):
            for b in range(VISITS):
                wide_ref[b, pl.ds(q * QUAD + j, ROWS, stride=PAD), :] = done[
                    j * ROWS:(j + 1) * ROWS, b * LANES:(b + 1) * LANES
                ]

    def two(i, carry):
        columns(2 * i + 1, odd_ref)
        rows(2 * i, even_ref)
        columns(2 * i + 2, even_ref)
        rows(2 * i + 1, odd_ref)
        return carry

    columns(0, even_ref)
    lax.fori_loop(0, QUADS // 2 - 1, two, 0)
    columns(QUADS - 1, odd_ref)
    rows(QUADS - 2, even_ref)
    rows(QUADS - 1, odd_ref)

    def gram_step(r, total):
        at = pl.multiple_of(r * PAD, PAD)
        pieces = [wide_ref[b, pl.ds(at, PAD), :].astype(BF16) for b in range(VISITS)]
        for b in range(VISITS):
            basis_ref[b, pl.ds(at, PAD), :] = pieces[b]
        images = jnp.concatenate(pieces, axis=1)
        return total + lax.dot_general(
            images, images, (((1,), (1,)), ((), ())), preferred_element_type=F32
        )

    gram = lax.fori_loop(0, ROWS, gram_step, jnp.zeros((PAD, PAD), F32), unroll=4)
    gram = jnp.concatenate([gram, jnp.zeros((PAD, LANES - PAD), F32)], axis=1)
    lane = iota((TILE, LANES), 1)
    part = gram[:TILE]
    part = jnp.where(lane >= TILE, pltpu.roll(gram[TILE:2 * TILE], TILE, 1), part)
    gram_ref[...] = jnp.where(lane >= 3 * TILE, pltpu.roll(gram[2 * TILE:], 3 * TILE, 1), part)


def moment_kernel(
    targets_hbm, gram_hbm, got_ref, basis_ref, science_ref, part_ref,
    targets_ref, hit_ref, gram_ref, sems,
):
    copies = fetch([(targets_hbm, targets_ref), (gram_hbm, gram_ref)], sems)
    gots = []
    for slot in range(2):
        got = got_ref[:, slot * SUB:(slot + 1) * SUB, :].astype(F32)
        gots.append(got.reshape(STRIPS // 2, 2 * COLS).astype(BF16))
    copies[0].wait()
    hits(targets_ref, hit_ref)
    science = jnp.zeros((ROWS, COLS), F32)
    for slot in range(2):
        got = gots[slot]
        for half in range(2):
            science = science + lax.dot_general(
                hit_ref[slot * 2 + half],
                got[:, half * COLS:(half + 1) * COLS],
                (((0,), (0,)), ((), ())),
                preferred_element_type=F32,
            )
    science_ref[...] = science

    def step(g, total):
        lines = science_ref[pl.ds(pl.multiple_of(g * SUB, SUB), SUB), :]
        for b in range(VISITS):
            for i in range(SUB):
                at = pl.multiple_of((g * SUB + i) * PAD, PAD)
                total = total + basis_ref[b, pl.ds(at, PAD), :].astype(F32) * lines[i:i + 1, b * LANES:(b + 1) * LANES]
        return total

    total = lax.fori_loop(0, ROWS // SUB, step, jnp.zeros((PAD, LANES), F32))
    moment = jnp.sum(total, axis=1, keepdims=True)
    copies[1].wait()
    lane = iota((TILE, LANES), 1)
    part = gram_ref[...]
    for i in range(3):
        part = jnp.where(lane == 6 * TILE + i, moment[i * TILE:(i + 1) * TILE], part)
    for v in range(part_ref.shape[0]):
        part_ref[v] = part


def solve_kernel(parts_ref, basis_ref, science_ref, diff_ref, coeff_ref):
    part = parts_ref[0]
    for i in range(1, parts_ref.shape[0]):
        part = part + parts_ref[i]
    lane = iota((PAD, LANES), 1)
    sub = iota((PAD, LANES), 0)
    lower = jnp.concatenate(
        [part, pltpu.roll(part, LANES - TILE, 1), pltpu.roll(part, LANES - 3 * TILE, 1)], axis=0
    )
    lower = jnp.where(lane // TILE <= sub // TILE, lower, 0.0)
    square = jnp.concatenate([lower, jnp.zeros((LANES - PAD, LANES), F32)], axis=0)
    system = jnp.where(lane // TILE > sub // TILE, square.T[:PAD], lower)
    moment = jnp.concatenate(
        [part[:, 6 * TILE + i:6 * TILE + i + 1] for i in range(3)], axis=0
    )
    system = jnp.where(lane == NB, moment, system)
    ahead = [jnp.broadcast_to(system[:, p:p + 1], (PAD, LANES)) for p in range(AHEAD)]
    for p in range(NB):
        column = ahead.pop(0)
        inverse = 1.0 / column[p:p + 1, :]
        here = sub == p

        def step(values):
            row = values[p:p + 1, :] * inverse
            return jnp.where(here, row, values - column * row)

        ahead = [step(values) for values in ahead]
        system = step(system)
        later = p + AHEAD
        if later <= NB:
            ahead.append(jnp.broadcast_to(system[:, later:later + 1], (PAD, LANES)))
    answer = ahead[0]
    coeff_ref[...] = jnp.sum(jnp.where(sub == lane, answer, 0.0), axis=0, keepdims=True)
    row = iota((SUB, LANES), 0)

    def step(g, carry):
        here = pl.ds(pl.multiple_of(g * SUB, SUB), SUB)
        for b in range(VISITS):
            sums = []
            for i in range(SUB):
                at = pl.multiple_of((g * SUB + i) * PAD, PAD)
                product = basis_ref[b, pl.ds(at, PAD), :].astype(F32) * answer
                total = product[:SUB]
                for n in range(1, PAD // SUB):
                    total = total + product[n * SUB:(n + 1) * SUB]
                sums.append(total)
            span = SUB // 2
            while span:
                keep = (row // span) % 2 == 0
                sums = [
                    jnp.where(keep, sums[i], sums[i + span])
                    + pltpu.roll(jnp.where(keep, sums[i + span], sums[i]), span, 0)
                    for i in range(span)
                ] if span == SUB // 2 else merge(sums, keep, span)
                span //= 2
            cut = slice(b * LANES, (b + 1) * LANES)
            diff_ref[here, cut] = science_ref[here, cut] - sums[0]
        return carry

    lax.fori_loop(0, ROWS // SUB, step, 0)


def merge(sums, keep, span):
    half = len(sums) // 2
    out = []
    for i in range(half):
        a, b = sums[i], sums[i + half]
        low = jnp.where(keep, a, b)
        high = jnp.where(keep, b, a)
        moved = jnp.where(keep, pltpu.roll(high, SUB - span, 0), pltpu.roll(high, span, 0))
        out.append(low + moved)
    return out


def share(block, axis):
    return lax.all_to_all(block, axis, 0, 0, tiled=True)


def body(template, science_src, target_rows, row_taps, col_taps):
    down = [(i, i + 1) for i in range(STRIPS - 1)]
    up = [(i + 1, i) for i in range(STRIPS - 1)]
    copied = jnp.broadcast_to(template[None], (VISITS, ROWS, LANES))
    tiles = share(copied, "visit")
    above = lax.ppermute(tiles, STRIP, down)
    below = lax.ppermute(tiles, STRIP, up)
    targets = target_rows.reshape(STRIPS // 2, 2 * SRC)
    (outgoing,) = call(
        prepare_kernel,
        [((STRIPS, TILE, LANES), BF16)],
        targets,
        science_src[0],
        scratch=[
            pltpu.VMEM(targets.shape, jnp.int32),
            pltpu.VMEM((SRC, COLS), BF16),
            pltpu.SemaphoreType.DMA((2,)),
        ],
        far=2,
    )
    incoming = share(outgoing, STRIP)
    basis, gram = call(
        basis_kernel,
        [((VISITS, ROWS * PAD, LANES), BF16), ((TILE, LANES), F32)],
        row_taps.T,
        col_taps.T,
        tiles,
        above,
        below,
        scratch=[
            pltpu.VMEM((TAPS, NB), BF16),
            pltpu.VMEM((TAPS, NB), BF16),
            pltpu.VMEM((VISITS, ROWS, LANES), BF16),
            pltpu.VMEM((LANES, LANES), F32),
            pltpu.VMEM((QUADS, QUAD * ROWS, 2 * LANES), BF16),
            pltpu.VMEM((PAD // 2, 2 * LANES, 2 * LANES), BF16),
            pltpu.VMEM((VISITS * FRAME, 2 * LANES), BF16),
            pltpu.VMEM((QUAD * FRAME, COLS), BF16),
            pltpu.VMEM((QUAD * FRAME, COLS), BF16),
            pltpu.VMEM((VISITS, ROWS * PAD, LANES), F32),
            pltpu.SemaphoreType.DMA((3,)),
        ],
        grant=24,
        far=3,
    )
    science, part = call(
        moment_kernel,
        [((ROWS, COLS), F32), ((VISITS, TILE, LANES), F32)],
        targets,
        gram,
        incoming,
        basis,
        scratch=[
            pltpu.VMEM(targets.shape, jnp.int32),
            pltpu.VMEM((4, STRIPS // 2, ROWS), BF16),
            pltpu.VMEM((TILE, LANES), F32),
            pltpu.SemaphoreType.DMA((2,)),
        ],
        far=2,
    )
    near = jnp.sum(share(part, ("x", "core")), axis=0)
    parts = share(jnp.broadcast_to(near[None], (VISITS, TILE, LANES)), "y")
    difference, coeffs = call(
        solve_kernel, [((ROWS, COLS), F32), ((1, LANES), F32)], parts, basis, science
    )
    return difference[None], coeffs[:, :NB]


def solution(mesh):
    sizes = (VISITS, 8, 4, 2)
    fine = Mesh(mesh.devices.reshape(sizes), ("visit",) + STRIP)
    in_specs = (P(STRIP, "visit"), P("visit", STRIP, None), P("visit", None), P(), P())
    out_specs = (P("visit", STRIP, None), P("visit", None))
    return jax.shard_map(body, mesh=fine, in_specs=in_specs, out_specs=out_specs, check_vma=False)
```

```python
import jax
import jax.numpy as jnp
from jax import lax
from jax.experimental import pallas as pl
from jax.experimental.pallas import tpu as pltpu
from jax.sharding import Mesh, PartitionSpec as P

STRIPS = 64
VISITS = 8
ROWS = 32
COLS = 1024
LANES = 128
SRC = 64
TAPS = 21
REACH = 10
NB = 45
PAD = 48
HALO = 16
FRAME = ROWS + 2 * HALO
OCT = 8
OCTS = PAD // OCT
SPAN = 16
SUB = 8
TILE = 16
AHEAD = 3
BIG = 1 << 20
F32 = jnp.float32
BF16 = jnp.bfloat16
STRIP = ("y", "x", "core")
MIB = 1 << 20


def vmem(count):
    return [pl.BlockSpec(memory_space=pltpu.VMEM)] * count


def iota(shape, dim):
    return lax.broadcasted_iota(jnp.int32, shape, dim)


def call(kernel, outs, *args, scratch=(), grant=8, far=0, stay=0):
    return pl.pallas_call(
        kernel,
        out_shape=tuple(
            pltpu.HBM(*o) if i < stay else jax.ShapeDtypeStruct(*o) for i, o in enumerate(outs)
        ),
        in_specs=[pl.BlockSpec(memory_space=pltpu.HBM)] * far + vmem(len(args) - far),
        out_specs=tuple(
            [pl.BlockSpec(memory_space=pltpu.HBM)] * stay + vmem(len(outs) - stay)
        ),
        scratch_shapes=list(scratch),
        compiler_params=pltpu.CompilerParams(vmem_limit_bytes=grant * MIB),
    )(*[pltpu.with_memory_space_constraint(arg, pltpu.HBM) for arg in args[:far]], *args[far:])


def my_strip():
    return (lax.axis_index("y") * 4 + lax.axis_index("x")) * 2 + lax.axis_index("core")


def fetch(pairs, sems):
    copies = [pltpu.make_async_copy(far, near, sems.at[i]) for i, (far, near) in enumerate(pairs)]
    for copy in copies:
        copy.start()
    return copies


def prepare_kernel(targets_hbm, src_hbm, out_ref, targets_ref, src_ref, sems):
    copies = fetch([(targets_hbm, targets_ref), (src_hbm, src_ref)], sems)
    for copy in copies:
        copy.wait()
    send(targets_ref, src_ref, out_ref)


def send(targets_ref, src_ref, out_ref):
    strip = my_strip()
    line = jnp.broadcast_to(targets_ref[pl.ds(strip // 2, 1), :], (SUB, LANES))
    line = pltpu.roll(line, (strip % 2) * SRC, 1)
    dest = line[:1, :SRC] // ROWS
    at_dest = dest == iota((STRIPS, SRC), 0)
    order = iota((STRIPS, SRC), 1)
    first = jnp.min(jnp.where(at_dest, order, BIG), axis=1, keepdims=True)
    last = jnp.max(jnp.where(at_dest, order, -1), axis=1, keepdims=True)
    src = src_ref[...]
    one = at_dest & (order == first)
    two = at_dest & (order == last) & (last != first)
    slots = []
    for pick in (one, two):
        rows = jnp.dot(pick.astype(F32).astype(BF16), src, preferred_element_type=F32)
        slots.append(rows.reshape(STRIPS, SUB, LANES))
    out_ref[...] = jnp.concatenate(slots, axis=1).astype(BF16)


def hits(targets_ref, hit_ref):
    strip = my_strip()
    targets = targets_ref[...]
    key = jnp.where(targets // ROWS == strip, (iota(targets.shape, 1) % SRC) * ROWS + targets % ROWS, BIG)
    swapped = jnp.where(key == BIG, -1, key)
    upper = iota(targets.shape, 1) >= SRC
    rows = iota((STRIPS // 2, ROWS), 1)
    for half in range(2):
        mine = upper if half else ~upper
        first = jnp.min(jnp.where(mine, key, BIG), axis=1, keepdims=True)
        last = jnp.max(jnp.where(mine, swapped, -1), axis=1, keepdims=True)
        one = (first < BIG) & (first % ROWS == rows)
        two = (last >= 0) & (last != first) & (last % ROWS == rows)
        hit_ref[half] = one.astype(F32).astype(BF16)
        hit_ref[2 + half] = two.astype(F32).astype(BF16)


def bands_kernel(
    row_hbm, col_hbm, row_band_ref, col_band_ref, row_ref, col_ref, spread_ref, sems
):
    for copy in fetch([(row_hbm, row_ref), (col_hbm, col_ref)], sems):
        copy.wait()
    bands(row_ref, col_ref, row_band_ref, col_band_ref, spread_ref)


def bands(row_ref, col_ref, row_band_ref, col_band_ref, spread_ref):
    spread_ref[...] = jnp.zeros((LANES, LANES), F32)
    spread_ref[HALO - REACH:HALO - REACH + TAPS, :NB] = row_ref[...].astype(F32)
    row_lines = spread_ref[...].T
    spread_ref[...] = jnp.zeros((LANES, LANES), F32)
    top = LANES // 2 + REACH
    col = col_ref[...].astype(F32)
    for t in range(TAPS):
        spread_ref[top - t:top - t + 1, :NB] = col[t:t + 1]
    col_lines = spread_ref[...].T
    above = iota((LANES, LANES), 1) <= iota((LANES, LANES), 0) - (LANES // 2 - REACH)
    for k in range(PAD):
        taps = jnp.broadcast_to(col_lines[k:k + 1], (LANES, LANES))
        wheel = pltpu.roll(taps, 0, 1, stride=1, stride_axis=0)
        cut = slice((k % 2) * LANES, (k % 2 + 1) * LANES)
        col_band_ref[k // 2, :LANES, cut] = jnp.where(above, wheel, 0.0).astype(BF16)
        col_band_ref[k // 2, LANES:, cut] = jnp.where(above, 0.0, wheel).astype(BF16)
    member = iota((2 * OCT, LANES), 0) % OCT
    for o in range(OCTS):
        lines = row_lines[o * OCT:(o + 1) * OCT]
        lines = jnp.where(member[:OCT] % 2 == 1, pltpu.roll(lines, FRAME, 1), lines)
        for r in range(0, ROWS, 2):
            moved = [pltpu.roll(lines, r + i, 1) if r + i else lines for i in range(2)]
            moved = jnp.concatenate(moved, axis=0)
            for t in range(OCT // 2):
                row_band_ref[o, r * OCT:(r + 2) * OCT, t * LANES:(t + 1) * LANES] = jnp.where(
                    member // 2 == t, moved, 0.0
                ).astype(BF16)


def basis_kernel(
    own_hbm, far_ref, near_ref, row_band_ref, col_band_ref,
    basis_ref, own_ref, win_ref, even_ref, odd_ref, wide_ref, sems,
):
    for copy in fetch([(own_hbm, own_ref)], sems):
        copy.wait()
    first = lax.axis_index("core") == 0
    zero = jnp.zeros((FRAME, LANES // 2), BF16)
    halves = [zero]
    for b in range(VISITS):
        above = jnp.where(first, far_ref[b, ROWS - HALO:, :], near_ref[b, ROWS - HALO:, :])
        below = jnp.where(first, near_ref[b, :HALO, :], far_ref[b, :HALO, :])
        block = jnp.concatenate([above, own_ref[b], below], axis=0)
        halves += [block[:, :LANES // 2], block[:, LANES // 2:]]
    halves.append(zero)
    shifted = [jnp.concatenate([halves[2 * i], halves[2 * i + 1]], axis=1) for i in range(VISITS + 1)]
    for b in range(VISITS):
        win_ref[b * FRAME:(b + 1) * FRAME, :LANES] = shifted[b]
        win_ref[b * FRAME:(b + 1) * FRAME, LANES:] = shifted[b + 1]

    def columns(q, smooth_ref):
        for pair in range(OCT // 2):
            both = jnp.dot(
                win_ref[...], col_band_ref[q * (OCT // 2) + pair], preferred_element_type=F32
            ).astype(BF16)
            for half in range(2):
                at = (pair * 2 + half) * FRAME
                for b in range(VISITS):
                    smooth_ref[at:at + FRAME, b * LANES:(b + 1) * LANES] = both[
                        b * FRAME:(b + 1) * FRAME, half * LANES:(half + 1) * LANES
                    ]

    def rows(q, smooth_ref):
        done = jnp.dot(row_band_ref[q], smooth_ref[...], preferred_element_type=F32)
        for r in range(ROWS):
            at = pl.multiple_of(r * PAD + q * OCT, OCT)
            for b in range(VISITS):
                wide_ref[b, pl.ds(at, OCT), :] = done[
                    r * OCT:(r + 1) * OCT, b * LANES:(b + 1) * LANES
                ]

    def two(i, carry):
        columns(2 * i + 1, odd_ref)
        rows(2 * i, even_ref)
        columns(2 * i + 2, even_ref)
        rows(2 * i + 1, odd_ref)
        return carry

    columns(0, even_ref)
    lax.fori_loop(0, OCTS // 2 - 1, two, 0)
    columns(OCTS - 1, odd_ref)
    rows(OCTS - 2, even_ref)
    rows(OCTS - 1, odd_ref)

    def gram_step(g, total):
        pieces = []
        for i in range(SPAN):
            at = pl.multiple_of((g * SPAN + i) * PAD, PAD)
            for b in range(VISITS):
                piece = wide_ref[b, pl.ds(at, PAD), :].astype(BF16)
                basis_ref[b, pl.ds(at, PAD), :] = piece
                pieces.append(piece)
        images = jnp.concatenate(pieces, axis=1)
        return total + lax.dot_general(
            images, images, (((1,), (1,)), ((), ())), preferred_element_type=F32
        )

    gram = lax.fori_loop(0, ROWS // SPAN, gram_step, jnp.zeros((PAD, PAD), F32))
    gram = jnp.concatenate([gram, jnp.zeros((PAD, LANES - PAD), F32)], axis=1)
    lane = iota((TILE, LANES), 1)
    part = gram[:TILE]
    part = jnp.where(lane >= TILE, pltpu.roll(gram[TILE:2 * TILE], TILE, 1), part)
    rest = jnp.where(lane >= 3 * TILE, pltpu.roll(gram[2 * TILE:], 3 * TILE, 1), part)
    for i in range(3):
        piece = rest.astype(BF16)
        basis_ref[0, ROWS * PAD + i * TILE:ROWS * PAD + (i + 1) * TILE, :] = piece
        rest = rest - piece.astype(F32)


def moment_kernel(
    targets_hbm, got_ref, basis_ref, science_hbm, part_ref, science_ref, targets_ref, hit_ref, sems
):
    copies = fetch([(targets_hbm, targets_ref)], sems)
    gots = []
    for slot in range(2):
        got = got_ref[:, slot * SUB:(slot + 1) * SUB, :].astype(F32)
        gots.append(got.reshape(STRIPS // 2, 2 * COLS).astype(BF16))
    copies[0].wait()
    hits(targets_ref, hit_ref)
    science = jnp.zeros((ROWS, COLS), F32)
    for slot in range(2):
        got = gots[slot]
        for half in range(2):
            science = science + lax.dot_general(
                hit_ref[slot * 2 + half],
                got[:, half * COLS:(half + 1) * COLS],
                (((0,), (0,)), ((), ())),
                preferred_element_type=F32,
            )
    science_ref[...] = science
    keep = pltpu.make_async_copy(science_ref, science_hbm, sems.at[1])
    keep.start()

    def step(g, total):
        lines = science_ref[pl.ds(pl.multiple_of(g * SUB, SUB), SUB), :]
        for b in range(VISITS):
            for i in range(SUB):
                at = pl.multiple_of((g * SUB + i) * PAD, PAD)
                total = total + basis_ref[b, pl.ds(at, PAD), :].astype(F32) * lines[i:i + 1, b * LANES:(b + 1) * LANES]
        return total

    total = lax.fori_loop(0, ROWS // SUB, step, jnp.zeros((PAD, LANES), F32))
    moment = jnp.sum(total, axis=1, keepdims=True)
    lane = iota((TILE, LANES), 1)
    part = jnp.zeros((TILE, LANES), F32)
    for i in (2, 1, 0):
        at = ROWS * PAD + i * TILE
        part = part + basis_ref[0, at:at + TILE, :].astype(F32)
    for i in range(3):
        part = jnp.where(lane == 6 * TILE + i, moment[i * TILE:(i + 1) * TILE], part)
    for v in range(part_ref.shape[0]):
        part_ref[v] = part
    keep.wait()


def solve_kernel(science_hbm, parts_ref, basis_ref, diff_ref, coeff_ref, science_ref, sems):
    copies = fetch([(science_hbm, science_ref)], sems)
    part = parts_ref[0]
    for i in range(1, parts_ref.shape[0]):
        part = part + parts_ref[i]
    lane = iota((PAD, LANES), 1)
    sub = iota((PAD, LANES), 0)
    lower = jnp.concatenate(
        [part, pltpu.roll(part, LANES - TILE, 1), pltpu.roll(part, LANES - 3 * TILE, 1)], axis=0
    )
    lower = jnp.where(lane // TILE <= sub // TILE, lower, 0.0)
    square = jnp.concatenate([lower, jnp.zeros((LANES - PAD, LANES), F32)], axis=0)
    system = jnp.where(lane // TILE > sub // TILE, square.T[:PAD], lower)
    moment = jnp.concatenate(
        [part[:, 6 * TILE + i:6 * TILE + i + 1] for i in range(3)], axis=0
    )
    system = jnp.where(lane == NB, moment, system)
    ahead = [jnp.broadcast_to(system[:, p:p + 1], (PAD, LANES)) for p in range(AHEAD)]
    for p in range(NB):
        column = ahead.pop(0)
        inverse = 1.0 / column[p:p + 1, :]
        here = sub == p

        def step(values):
            row = values[p:p + 1, :] * inverse
            return jnp.where(here, row, values - column * row)

        ahead = [step(values) for values in ahead]
        system = step(system)
        later = p + AHEAD
        if later <= NB:
            ahead.append(jnp.broadcast_to(system[:, later:later + 1], (PAD, LANES)))
    answer = ahead[0]
    coeff_ref[...] = jnp.sum(jnp.where(sub == lane, answer, 0.0), axis=0, keepdims=True)
    row = iota((SUB, LANES), 0)
    copies[0].wait()

    def step(g, carry):
        here = pl.ds(pl.multiple_of(g * SUB, SUB), SUB)
        for b in range(VISITS):
            sums = []
            for i in range(SUB):
                at = pl.multiple_of((g * SUB + i) * PAD, PAD)
                product = basis_ref[b, pl.ds(at, PAD), :].astype(F32) * answer
                total = product[:SUB]
                for n in range(1, PAD // SUB):
                    total = total + product[n * SUB:(n + 1) * SUB]
                sums.append(total)
            span = SUB // 2
            while span:
                keep = (row // span) % 2 == 0
                sums = [
                    jnp.where(keep, sums[i], sums[i + span])
                    + pltpu.roll(jnp.where(keep, sums[i + span], sums[i]), span, 0)
                    for i in range(span)
                ] if span == SUB // 2 else merge(sums, keep, span)
                span //= 2
            cut = slice(b * LANES, (b + 1) * LANES)
            diff_ref[here, cut] = science_ref[here, cut] - sums[0]
        return carry

    lax.fori_loop(0, ROWS // SUB, step, 0)


def merge(sums, keep, span):
    half = len(sums) // 2
    out = []
    for i in range(half):
        a, b = sums[i], sums[i + half]
        low = jnp.where(keep, a, b)
        high = jnp.where(keep, b, a)
        moved = jnp.where(keep, pltpu.roll(high, SUB - span, 0), pltpu.roll(high, span, 0))
        out.append(low + moved)
    return out


def share(block, axis):
    return lax.all_to_all(block, axis, 0, 0, tiled=True)


def body(template, science_src, target_rows, row_taps, col_taps):
    inner = [(i, i ^ 1) for i in range(STRIPS)]
    outer = [(i, i + 1 if i % 2 else i - 1) for i in range(1, STRIPS - 1)]
    copied = jnp.broadcast_to(template[None], (VISITS, ROWS, LANES))
    tiles = share(copied, "visit")
    targets = target_rows.reshape(STRIPS // 2, 2 * SRC)
    (outgoing,) = call(
        prepare_kernel,
        [((STRIPS, TILE, LANES), BF16)],
        targets,
        science_src[0],
        scratch=[
            pltpu.VMEM(targets.shape, jnp.int32),
            pltpu.VMEM((SRC, COLS), BF16),
            pltpu.SemaphoreType.DMA((2,)),
        ],
        far=2,
    )
    incoming = share(outgoing, STRIP)
    far_tiles = lax.ppermute(tiles, STRIP, outer)
    near_tiles = lax.ppermute(tiles, STRIP, inner)
    row_bands, col_bands = call(
        bands_kernel,
        [((OCTS, OCT * ROWS, OCT * FRAME), BF16), ((PAD // 2, 2 * LANES, 2 * LANES), BF16)],
        row_taps.T,
        col_taps.T,
        scratch=[
            pltpu.VMEM((TAPS, NB), BF16),
            pltpu.VMEM((TAPS, NB), BF16),
            pltpu.VMEM((LANES, LANES), F32),
            pltpu.SemaphoreType.DMA((2,)),
        ],
        far=2,
    )
    (basis,) = call(
        basis_kernel,
        [((VISITS, ROWS * PAD + 3 * TILE, LANES), BF16)],
        tiles,
        far_tiles,
        near_tiles,
        row_bands,
        col_bands,
        scratch=[
            pltpu.VMEM((VISITS, ROWS, LANES), BF16),
            pltpu.VMEM((VISITS * FRAME, 2 * LANES), BF16),
            pltpu.VMEM((OCT * FRAME, COLS), BF16),
            pltpu.VMEM((OCT * FRAME, COLS), BF16),
            pltpu.VMEM((VISITS, ROWS * PAD, LANES), F32),
            pltpu.SemaphoreType.DMA((1,)),
        ],
        grant=24,
        far=1,
    )
    science, part = call(
        moment_kernel,
        [((ROWS, COLS), F32), ((VISITS, TILE, LANES), F32)],
        targets,
        incoming,
        basis,
        scratch=[
            pltpu.VMEM((ROWS, COLS), F32),
            pltpu.VMEM(targets.shape, jnp.int32),
            pltpu.VMEM((4, STRIPS // 2, ROWS), BF16),
            pltpu.SemaphoreType.DMA((2,)),
        ],
        far=1,
        stay=1,
    )
    near = jnp.sum(share(part, ("x", "core")), axis=0)
    parts = share(jnp.broadcast_to(near[None], (VISITS, TILE, LANES)), "y")
    difference, coeffs = call(
        solve_kernel,
        [((ROWS, COLS), F32), ((1, LANES), F32)],
        science,
        parts,
        basis,
        scratch=[pltpu.VMEM((ROWS, COLS), F32), pltpu.SemaphoreType.DMA((1,))],
        far=1,
    )
    return difference[None], coeffs[:, :NB]


def solution(mesh):
    sizes = (VISITS, 8, 4, 2)
    fine = Mesh(mesh.devices.reshape(sizes), ("visit",) + STRIP)
    in_specs = (P(STRIP, "visit"), P("visit", STRIP, None), P("visit", None), P(), P())
    out_specs = (P("visit", STRIP, None), P("visit", None))
    return jax.shard_map(body, mesh=fine, in_specs=in_specs, out_specs=out_specs, check_vma=False)
```

```python
import jax
import jax.numpy as jnp
from jax import lax
from jax.experimental import pallas as pl
from jax.experimental.pallas import tpu as pltpu
from jax.sharding import Mesh, PartitionSpec as P

STRIPS = 64
VISITS = 8
ROWS = 32
COLS = 1024
LANES = 128
SRC = 64
TAPS = 21
REACH = 10
NB = 45
PAD = 48
HALO = 16
FRAME = ROWS + 2 * HALO
OCT = 8
OCTS = PAD // OCT
SPAN = 16
SUB = 8
TILE = 16
AHEAD = 8
BIG = 1 << 20
F32 = jnp.float32
BF16 = jnp.bfloat16
STRIP = ("y", "x", "core")
MIB = 1 << 20


def vmem(count):
    return [pl.BlockSpec(memory_space=pltpu.VMEM)] * count


def iota(shape, dim):
    return lax.broadcasted_iota(jnp.int32, shape, dim)


def call(kernel, outs, *args, scratch=(), grant=8, far=0, stay=0):
    return pl.pallas_call(
        kernel,
        out_shape=tuple(
            pltpu.HBM(*o) if i < stay else jax.ShapeDtypeStruct(*o) for i, o in enumerate(outs)
        ),
        in_specs=[pl.BlockSpec(memory_space=pltpu.HBM)] * far + vmem(len(args) - far),
        out_specs=tuple(
            [pl.BlockSpec(memory_space=pltpu.HBM)] * stay + vmem(len(outs) - stay)
        ),
        scratch_shapes=list(scratch),
        compiler_params=pltpu.CompilerParams(vmem_limit_bytes=grant * MIB),
    )(*[pltpu.with_memory_space_constraint(arg, pltpu.HBM) for arg in args[:far]], *args[far:])


def my_strip():
    return (lax.axis_index("y") * 4 + lax.axis_index("x")) * 2 + lax.axis_index("core")


def fetch(pairs, sems):
    copies = [pltpu.make_async_copy(far, near, sems.at[i]) for i, (far, near) in enumerate(pairs)]
    for copy in copies:
        copy.start()
    return copies


def prepare_kernel(targets_hbm, src_hbm, out_ref, targets_ref, src_ref, sems):
    copies = fetch([(targets_hbm, targets_ref), (src_hbm, src_ref)], sems)
    for copy in copies:
        copy.wait()
    send(targets_ref, src_ref, out_ref)


def send(targets_ref, src_ref, out_ref):
    strip = my_strip()
    line = jnp.broadcast_to(targets_ref[pl.ds(strip // 2, 1), :], (SUB, LANES))
    line = pltpu.roll(line, (strip % 2) * SRC, 1)
    dest = line[:1, :SRC] // ROWS
    at_dest = dest == iota((STRIPS, SRC), 0)
    order = iota((STRIPS, SRC), 1)
    first = jnp.min(jnp.where(at_dest, order, BIG), axis=1, keepdims=True)
    last = jnp.max(jnp.where(at_dest, order, -1), axis=1, keepdims=True)
    src = src_ref[...]
    one = at_dest & (order == first)
    two = at_dest & (order == last) & (last != first)
    slots = []
    for pick in (one, two):
        rows = jnp.dot(pick.astype(F32).astype(BF16), src, preferred_element_type=F32)
        slots.append(rows.reshape(STRIPS, SUB, LANES))
    out_ref[...] = jnp.concatenate(slots, axis=1).astype(BF16)


def hits(targets_ref, hit_ref):
    strip = my_strip()
    targets = targets_ref[...]
    key = jnp.where(targets // ROWS == strip, (iota(targets.shape, 1) % SRC) * ROWS + targets % ROWS, BIG)
    swapped = jnp.where(key == BIG, -1, key)
    upper = iota(targets.shape, 1) >= SRC
    rows = iota((STRIPS // 2, ROWS), 1)
    for half in range(2):
        mine = upper if half else ~upper
        first = jnp.min(jnp.where(mine, key, BIG), axis=1, keepdims=True)
        last = jnp.max(jnp.where(mine, swapped, -1), axis=1, keepdims=True)
        one = (first < BIG) & (first % ROWS == rows)
        two = (last >= 0) & (last != first) & (last % ROWS == rows)
        blank = jnp.zeros((STRIPS // 2, LANES - ROWS), F32)
        for slot, pick in enumerate((one, two)):
            pick = jnp.concatenate([pick.astype(F32), blank], axis=1)
            hit_ref[slot * 2 + half] = pick.astype(BF16)


def bands_kernel(
    row_hbm, col_hbm, targets_hbm, row_band_ref, col_band_ref, hit_ref,
    row_ref, col_ref, targets_ref, spread_ref, sems,
):
    for copy in fetch([(row_hbm, row_ref), (col_hbm, col_ref), (targets_hbm, targets_ref)], sems):
        copy.wait()
    hits(targets_ref, hit_ref)
    bands(row_ref, col_ref, row_band_ref, col_band_ref, spread_ref)


def bands(row_ref, col_ref, row_band_ref, col_band_ref, spread_ref):
    spread_ref[...] = jnp.zeros((LANES, LANES), F32)
    spread_ref[HALO - REACH:HALO - REACH + TAPS, :NB] = row_ref[...].astype(F32)
    row_lines = spread_ref[...].T
    spread_ref[...] = jnp.zeros((LANES, LANES), F32)
    top = LANES // 2 + REACH
    col = col_ref[...].astype(F32)
    for t in range(TAPS):
        spread_ref[top - t:top - t + 1, :NB] = col[t:t + 1]
    col_lines = spread_ref[...].T
    above = iota((LANES, LANES), 1) <= iota((LANES, LANES), 0) - (LANES // 2 - REACH)
    for k in range(PAD):
        taps = jnp.broadcast_to(col_lines[k:k + 1], (LANES, LANES))
        wheel = pltpu.roll(taps, 0, 1, stride=1, stride_axis=0)
        cut = slice((k % 2) * LANES, (k % 2 + 1) * LANES)
        col_band_ref[k // 2, :LANES, cut] = jnp.where(above, wheel, 0.0).astype(BF16)
        col_band_ref[k // 2, LANES:, cut] = jnp.where(above, 0.0, wheel).astype(BF16)
    member = iota((2 * OCT, LANES), 0) % OCT
    for o in range(OCTS):
        lines = row_lines[o * OCT:(o + 1) * OCT]
        lines = jnp.where(member[:OCT] % 2 == 1, pltpu.roll(lines, FRAME, 1), lines)
        for r in range(0, ROWS, 2):
            moved = [pltpu.roll(lines, r + i, 1) if r + i else lines for i in range(2)]
            moved = jnp.concatenate(moved, axis=0)
            for t in range(OCT // 2):
                row_band_ref[o, r * OCT:(r + 2) * OCT, t * LANES:(t + 1) * LANES] = jnp.where(
                    member // 2 == t, moved, 0.0
                ).astype(BF16)


def basis_kernel(
    own_hbm, far_ref, near_ref, row_band_ref, col_band_ref, hit_ref,
    basis_ref, own_ref, win_ref, even_ref, odd_ref, wide_ref, sems,
):
    copies = fetch([(own_hbm, own_ref)], sems)
    for i in range(4):
        basis_ref[1 + i, ROWS * PAD:ROWS * PAD + STRIPS // 2, :] = hit_ref[i]
    copies[0].wait()
    first = lax.axis_index("core") == 0
    zero = jnp.zeros((FRAME, LANES // 2), BF16)
    halves = [zero]
    for b in range(VISITS):
        above = jnp.where(first, far_ref[b, ROWS - HALO:, :], near_ref[b, ROWS - HALO:, :])
        below = jnp.where(first, near_ref[b, :HALO, :], far_ref[b, :HALO, :])
        block = jnp.concatenate([above, own_ref[b], below], axis=0)
        halves += [block[:, :LANES // 2], block[:, LANES // 2:]]
    halves.append(zero)
    shifted = [jnp.concatenate([halves[2 * i], halves[2 * i + 1]], axis=1) for i in range(VISITS + 1)]
    for b in range(VISITS):
        win_ref[b * FRAME:(b + 1) * FRAME, :LANES] = shifted[b]
        win_ref[b * FRAME:(b + 1) * FRAME, LANES:] = shifted[b + 1]

    def columns(q, smooth_ref):
        for pair in range(OCT // 2):
            both = jnp.dot(
                win_ref[...], col_band_ref[q * (OCT // 2) + pair], preferred_element_type=F32
            ).astype(BF16)
            for half in range(2):
                at = (pair * 2 + half) * FRAME
                for b in range(VISITS):
                    smooth_ref[at:at + FRAME, b * LANES:(b + 1) * LANES] = both[
                        b * FRAME:(b + 1) * FRAME, half * LANES:(half + 1) * LANES
                    ]

    def rows(q, smooth_ref):
        done = jnp.dot(row_band_ref[q], smooth_ref[...], preferred_element_type=F32)
        for r in range(ROWS):
            at = pl.multiple_of(r * PAD + q * OCT, OCT)
            for b in range(VISITS):
                wide_ref[b, pl.ds(at, OCT), :] = done[
                    r * OCT:(r + 1) * OCT, b * LANES:(b + 1) * LANES
                ]

    def two(i, carry):
        columns(2 * i + 1, odd_ref)
        rows(2 * i, even_ref)
        columns(2 * i + 2, even_ref)
        rows(2 * i + 1, odd_ref)
        return carry

    columns(0, even_ref)
    lax.fori_loop(0, OCTS // 2 - 1, two, 0)
    columns(OCTS - 1, odd_ref)
    rows(OCTS - 2, even_ref)
    rows(OCTS - 1, odd_ref)

    def gram_step(g, total):
        pieces = []
        for i in range(SPAN):
            at = pl.multiple_of((g * SPAN + i) * PAD, PAD)
            for b in range(VISITS):
                piece = wide_ref[b, pl.ds(at, PAD), :].astype(BF16)
                basis_ref[b, pl.ds(at, PAD), :] = piece
                pieces.append(piece)
        images = jnp.concatenate(pieces, axis=1)
        return total + lax.dot_general(
            images, images, (((1,), (1,)), ((), ())), preferred_element_type=F32
        )

    gram = lax.fori_loop(0, ROWS // SPAN, gram_step, jnp.zeros((PAD, PAD), F32))
    gram = jnp.concatenate([gram, jnp.zeros((PAD, LANES - PAD), F32)], axis=1)
    lane = iota((TILE, LANES), 1)
    part = gram[:TILE]
    part = jnp.where(lane >= TILE, pltpu.roll(gram[TILE:2 * TILE], TILE, 1), part)
    rest = jnp.where(lane >= 3 * TILE, pltpu.roll(gram[2 * TILE:], 3 * TILE, 1), part)
    for i in range(3):
        piece = rest.astype(BF16)
        basis_ref[0, ROWS * PAD + i * TILE:ROWS * PAD + (i + 1) * TILE, :] = piece
        rest = rest - piece.astype(F32)


def moment_kernel(
    got_ref, basis_ref, science_hbm, part_ref, science_ref, sem
):
    gots = []
    for slot in range(2):
        got = got_ref[:, slot * SUB:(slot + 1) * SUB, :].astype(F32)
        gots.append(got.reshape(STRIPS // 2, 2 * COLS).astype(BF16))
    science = jnp.zeros((ROWS, COLS), F32)
    for slot in range(2):
        got = gots[slot]
        for half in range(2):
            science = science + lax.dot_general(
                basis_ref[1 + slot * 2 + half, ROWS * PAD:ROWS * PAD + STRIPS // 2, :ROWS],
                got[:, half * COLS:(half + 1) * COLS],
                (((0,), (0,)), ((), ())),
                preferred_element_type=F32,
            )
    science_ref[...] = science
    keep = pltpu.make_async_copy(science_ref, science_hbm, sem)
    keep.start()

    def step(g, total):
        lines = science_ref[pl.ds(pl.multiple_of(g * SUB, SUB), SUB), :]
        for b in range(VISITS):
            for i in range(SUB):
                at = pl.multiple_of((g * SUB + i) * PAD, PAD)
                total = total + basis_ref[b, pl.ds(at, PAD), :].astype(F32) * lines[i:i + 1, b * LANES:(b + 1) * LANES]
        return total

    total = lax.fori_loop(0, ROWS // SUB, step, jnp.zeros((PAD, LANES), F32))
    moment = jnp.sum(total, axis=1, keepdims=True)
    lane = iota((TILE, LANES), 1)
    part = jnp.zeros((TILE, LANES), F32)
    for i in (2, 1, 0):
        at = ROWS * PAD + i * TILE
        part = part + basis_ref[0, at:at + TILE, :].astype(F32)
    for i in range(3):
        part = jnp.where(lane == 6 * TILE + i, moment[i * TILE:(i + 1) * TILE], part)
    for v in range(part_ref.shape[0]):
        part_ref[v] = part
    keep.wait()


def solve_kernel(science_hbm, parts_ref, basis_ref, diff_ref, coeff_ref, science_ref, sems):
    copies = fetch([(science_hbm, science_ref)], sems)
    part = parts_ref[0]
    for i in range(1, parts_ref.shape[0]):
        part = part + parts_ref[i]
    lane = iota((PAD, LANES), 1)
    sub = iota((PAD, LANES), 0)
    lower = jnp.concatenate(
        [part, pltpu.roll(part, LANES - TILE, 1), pltpu.roll(part, LANES - 3 * TILE, 1)], axis=0
    )
    lower = jnp.where(lane // TILE <= sub // TILE, lower, 0.0)
    square = jnp.concatenate([lower, jnp.zeros((LANES - PAD, LANES), F32)], axis=0)
    system = jnp.where(lane // TILE > sub // TILE, square.T[:PAD], lower)
    moment = jnp.concatenate(
        [part[:, 6 * TILE + i:6 * TILE + i + 1] for i in range(3)], axis=0
    )
    system = jnp.where(lane == NB, moment, system)
    ahead = [jnp.broadcast_to(system[:, p:p + 1], (PAD, LANES)) for p in range(AHEAD)]
    for p in range(NB):
        column = ahead.pop(0)
        inverse = 1.0 / column[p:p + 1, :]
        here = sub == p

        def step(values):
            row = values[p:p + 1, :] * inverse
            return jnp.where(here, row, values - column * row)

        ahead = [step(values) for values in ahead]
        system = step(system)
        later = p + AHEAD
        if later <= NB:
            ahead.append(jnp.broadcast_to(system[:, later:later + 1], (PAD, LANES)))
    answer = ahead[0]
    coeff_ref[...] = jnp.sum(jnp.where(sub == lane, answer, 0.0), axis=0, keepdims=True)
    row = iota((SUB, LANES), 0)
    copies[0].wait()

    def step(g, carry):
        here = pl.ds(pl.multiple_of(g * SUB, SUB), SUB)
        for b in range(VISITS):
            sums = []
            for i in range(SUB):
                at = pl.multiple_of((g * SUB + i) * PAD, PAD)
                product = basis_ref[b, pl.ds(at, PAD), :].astype(F32) * answer
                total = product[:SUB]
                for n in range(1, PAD // SUB):
                    total = total + product[n * SUB:(n + 1) * SUB]
                sums.append(total)
            span = SUB // 2
            while span:
                keep = (row // span) % 2 == 0
                sums = [
                    jnp.where(keep, sums[i], sums[i + span])
                    + pltpu.roll(jnp.where(keep, sums[i + span], sums[i]), span, 0)
                    for i in range(span)
                ] if span == SUB // 2 else merge(sums, keep, span)
                span //= 2
            cut = slice(b * LANES, (b + 1) * LANES)
            diff_ref[here, cut] = science_ref[here, cut] - sums[0]
        return carry

    lax.fori_loop(0, ROWS // SUB, step, 0)


def merge(sums, keep, span):
    half = len(sums) // 2
    out = []
    for i in range(half):
        a, b = sums[i], sums[i + half]
        low = jnp.where(keep, a, b)
        high = jnp.where(keep, b, a)
        moved = jnp.where(keep, pltpu.roll(high, SUB - span, 0), pltpu.roll(high, span, 0))
        out.append(low + moved)
    return out


def share(block, axis):
    return lax.all_to_all(block, axis, 0, 0, tiled=True)


def body(template, science_src, target_rows, row_taps, col_taps):
    inner = [(i, i ^ 1) for i in range(STRIPS)]
    outer = [(i, i + 1 if i % 2 else i - 1) for i in range(1, STRIPS - 1)]
    copied = jnp.broadcast_to(template[None], (VISITS, ROWS, LANES))
    tiles = share(copied, "visit")
    targets = target_rows.reshape(STRIPS // 2, 2 * SRC)
    (outgoing,) = call(
        prepare_kernel,
        [((STRIPS, TILE, LANES), BF16)],
        targets,
        science_src[0],
        scratch=[
            pltpu.VMEM(targets.shape, jnp.int32),
            pltpu.VMEM((SRC, COLS), BF16),
            pltpu.SemaphoreType.DMA((2,)),
        ],
        far=2,
    )
    incoming = share(outgoing, STRIP)
    far_tiles = lax.ppermute(tiles, STRIP, outer)
    near_tiles = lax.ppermute(tiles, STRIP, inner)
    row_bands, col_bands, hit = call(
        bands_kernel,
        [((OCTS, OCT * ROWS, OCT * FRAME), BF16), ((PAD // 2, 2 * LANES, 2 * LANES), BF16), ((4, STRIPS // 2, LANES), BF16)],
        row_taps.T,
        col_taps.T,
        targets,
        scratch=[
            pltpu.VMEM((TAPS, NB), BF16),
            pltpu.VMEM((TAPS, NB), BF16),
            pltpu.VMEM(targets.shape, jnp.int32),
            pltpu.VMEM((LANES, LANES), F32),
            pltpu.SemaphoreType.DMA((3,)),
        ],
        far=3,
    )
    (basis,) = call(
        basis_kernel,
        [((VISITS, ROWS * PAD + 3 * TILE, LANES), BF16)],
        tiles,
        far_tiles,
        near_tiles,
        row_bands,
        col_bands,
        hit,
        scratch=[
            pltpu.VMEM((VISITS, ROWS, LANES), BF16),
            pltpu.VMEM((VISITS * FRAME, 2 * LANES), BF16),
            pltpu.VMEM((OCT * FRAME, COLS), BF16),
            pltpu.VMEM((OCT * FRAME, COLS), BF16),
            pltpu.VMEM((VISITS, ROWS * PAD, LANES), F32),
            pltpu.SemaphoreType.DMA((1,)),
        ],
        grant=24,
        far=1,
    )
    science, part = call(
        moment_kernel,
        [((ROWS, COLS), F32), ((VISITS, TILE, LANES), F32)],
        incoming,
        basis,
        scratch=[pltpu.VMEM((ROWS, COLS), F32), pltpu.SemaphoreType.DMA],
        stay=1,
    )
    near = jnp.sum(share(part, ("x", "core")), axis=0)
    parts = share(jnp.broadcast_to(near[None], (VISITS, TILE, LANES)), "y")
    difference, coeffs = call(
        solve_kernel,
        [((ROWS, COLS), F32), ((1, LANES), F32)],
        science,
        parts,
        basis,
        scratch=[pltpu.VMEM((ROWS, COLS), F32), pltpu.SemaphoreType.DMA((1,))],
        far=1,
    )
    return difference[None], coeffs[:, :NB]


def solution(mesh):
    sizes = (VISITS, 8, 4, 2)
    fine = Mesh(mesh.devices.reshape(sizes), ("visit",) + STRIP)
    in_specs = (P(STRIP, "visit"), P("visit", STRIP, None), P("visit", None), P(), P())
    out_specs = (P("visit", STRIP, None), P("visit", None))
    return jax.shard_map(body, mesh=fine, in_specs=in_specs, out_specs=out_specs, check_vma=False)
```

```python
import jax
import jax.numpy as jnp
from jax import lax
from jax.experimental import pallas as pl
from jax.experimental.pallas import tpu as pltpu
from jax.sharding import Mesh, PartitionSpec as P

STRIPS = 64
VISITS = 8
ROWS = 32
COLS = 1024
LANES = 128
SRC = 64
TAPS = 21
REACH = 10
NB = 45
PAD = 48
HALO = 16
FRAME = ROWS + 2 * HALO
OCT = 8
OCTS = PAD // OCT
SPAN = 32
SUB = 8
TILE = 16
AHEAD = 8
BIG = 1 << 20
F32 = jnp.float32
BF16 = jnp.bfloat16
STRIP = ("y", "x", "core")
MIB = 1 << 20


def vmem(count):
    return [pl.BlockSpec(memory_space=pltpu.VMEM)] * count


def iota(shape, dim):
    return lax.broadcasted_iota(jnp.int32, shape, dim)


def call(kernel, outs, *args, scratch=(), grant=8, far=0, stay=0):
    return pl.pallas_call(
        kernel,
        out_shape=tuple(
            pltpu.HBM(*o) if i < stay else jax.ShapeDtypeStruct(*o) for i, o in enumerate(outs)
        ),
        in_specs=[pl.BlockSpec(memory_space=pltpu.HBM)] * far + vmem(len(args) - far),
        out_specs=tuple(
            [pl.BlockSpec(memory_space=pltpu.HBM)] * stay + vmem(len(outs) - stay)
        ),
        scratch_shapes=list(scratch),
        compiler_params=pltpu.CompilerParams(vmem_limit_bytes=grant * MIB),
    )(*[pltpu.with_memory_space_constraint(arg, pltpu.HBM) for arg in args[:far]], *args[far:])


def my_strip():
    return (lax.axis_index("y") * 4 + lax.axis_index("x")) * 2 + lax.axis_index("core")


def fetch(pairs, sems):
    copies = [pltpu.make_async_copy(far, near, sems.at[i]) for i, (far, near) in enumerate(pairs)]
    for copy in copies:
        copy.start()
    return copies


def prepare_kernel(targets_hbm, src_hbm, out_ref, targets_ref, src_ref, sems):
    copies = fetch([(targets_hbm, targets_ref), (src_hbm, src_ref)], sems)
    for copy in copies:
        copy.wait()
    send(targets_ref, src_ref, out_ref)


def send(targets_ref, src_ref, out_ref):
    strip = my_strip()
    line = jnp.broadcast_to(targets_ref[pl.ds(strip // 2, 1), :], (SUB, LANES))
    line = pltpu.roll(line, (strip % 2) * SRC, 1)
    dest = line[:1, :SRC] // ROWS
    at_dest = dest == iota((STRIPS, SRC), 0)
    order = iota((STRIPS, SRC), 1)
    first = jnp.min(jnp.where(at_dest, order, BIG), axis=1, keepdims=True)
    last = jnp.max(jnp.where(at_dest, order, -1), axis=1, keepdims=True)
    src = src_ref[...]
    one = at_dest & (order == first)
    two = at_dest & (order == last) & (last != first)
    slots = []
    for pick in (one, two):
        rows = jnp.dot(pick.astype(F32).astype(BF16), src, preferred_element_type=F32)
        slots.append(rows.reshape(STRIPS, SUB, LANES))
    out_ref[...] = jnp.concatenate(slots, axis=1).astype(BF16)


def hits(targets_ref, hit_ref):
    strip = my_strip()
    targets = targets_ref[...]
    key = jnp.where(targets // ROWS == strip, (iota(targets.shape, 1) % SRC) * ROWS + targets % ROWS, BIG)
    swapped = jnp.where(key == BIG, -1, key)
    upper = iota(targets.shape, 1) >= SRC
    rows = iota((STRIPS // 2, ROWS), 1)
    for half in range(2):
        mine = upper if half else ~upper
        first = jnp.min(jnp.where(mine, key, BIG), axis=1, keepdims=True)
        last = jnp.max(jnp.where(mine, swapped, -1), axis=1, keepdims=True)
        one = (first < BIG) & (first % ROWS == rows)
        two = (last >= 0) & (last != first) & (last % ROWS == rows)
        blank = jnp.zeros((STRIPS // 2, LANES - ROWS), F32)
        for slot, pick in enumerate((one, two)):
            pick = jnp.concatenate([pick.astype(F32), blank], axis=1)
            hit_ref[slot * 2 + half] = pick.astype(BF16)


def bands_kernel(
    row_hbm, col_hbm, targets_hbm, own_hbm, row_band_ref, col_band_ref, hit_ref, own_ref,
    row_ref, col_ref, targets_ref, spread_ref, sems,
):
    copies = fetch(
        [(row_hbm, row_ref), (col_hbm, col_ref), (targets_hbm, targets_ref), (own_hbm, own_ref)],
        sems,
    )
    for copy in copies:
        copy.wait()
    hits(targets_ref, hit_ref)
    bands(row_ref, col_ref, row_band_ref, col_band_ref, spread_ref)


def bands(row_ref, col_ref, row_band_ref, col_band_ref, spread_ref):
    spread_ref[...] = jnp.zeros((LANES, LANES), F32)
    spread_ref[HALO - REACH:HALO - REACH + TAPS, :NB] = row_ref[...].astype(F32)
    row_lines = spread_ref[...].T
    spread_ref[...] = jnp.zeros((LANES, LANES), F32)
    top = LANES // 2 + REACH
    col = col_ref[...].astype(F32)
    for t in range(TAPS):
        spread_ref[top - t:top - t + 1, :NB] = col[t:t + 1]
    col_lines = spread_ref[...].T
    above = iota((LANES, LANES), 1) <= iota((LANES, LANES), 0) - (LANES // 2 - REACH)
    for k in range(PAD):
        taps = jnp.broadcast_to(col_lines[k:k + 1], (LANES, LANES))
        wheel = pltpu.roll(taps, 0, 1, stride=1, stride_axis=0)
        cut = slice((k % 2) * LANES, (k % 2 + 1) * LANES)
        col_band_ref[k // 2, :LANES, cut] = jnp.where(above, wheel, 0.0).astype(BF16)
        col_band_ref[k // 2, LANES:, cut] = jnp.where(above, 0.0, wheel).astype(BF16)
    member = iota((2 * OCT, LANES), 0) % OCT
    for o in range(OCTS):
        lines = row_lines[o * OCT:(o + 1) * OCT]
        lines = jnp.where(member[:OCT] % 2 == 1, pltpu.roll(lines, FRAME, 1), lines)
        for r in range(0, ROWS, 2):
            moved = [pltpu.roll(lines, r + i, 1) if r + i else lines for i in range(2)]
            moved = jnp.concatenate(moved, axis=0)
            for t in range(OCT // 2):
                row_band_ref[o, r * OCT:(r + 2) * OCT, t * LANES:(t + 1) * LANES] = jnp.where(
                    member // 2 == t, moved, 0.0
                ).astype(BF16)


def basis_kernel(
    own_ref, far_ref, near_ref, row_band_ref, col_band_ref, hit_ref,
    basis_ref, win_ref, even_ref, odd_ref, wide_ref,
):
    for i in range(4):
        basis_ref[1 + i, ROWS * PAD:ROWS * PAD + STRIPS // 2, :] = hit_ref[i]
    first = lax.axis_index("core") == 0
    zero = jnp.zeros((FRAME, LANES // 2), BF16)
    halves = [zero]
    for b in range(VISITS):
        above = jnp.where(first, far_ref[b, ROWS - HALO:, :], near_ref[b, ROWS - HALO:, :])
        below = jnp.where(first, near_ref[b, :HALO, :], far_ref[b, :HALO, :])
        block = jnp.concatenate([above, own_ref[b], below], axis=0)
        halves += [block[:, :LANES // 2], block[:, LANES // 2:]]
    halves.append(zero)
    shifted = [jnp.concatenate([halves[2 * i], halves[2 * i + 1]], axis=1) for i in range(VISITS + 1)]
    for b in range(VISITS):
        win_ref[b * FRAME:(b + 1) * FRAME, :LANES] = shifted[b]
        win_ref[b * FRAME:(b + 1) * FRAME, LANES:] = shifted[b + 1]

    def columns(q, smooth_ref):
        for pair in range(OCT // 2):
            both = jnp.dot(
                win_ref[...], col_band_ref[q * (OCT // 2) + pair], preferred_element_type=F32
            ).astype(BF16)
            for half in range(2):
                at = (pair * 2 + half) * FRAME
                for b in range(VISITS):
                    smooth_ref[at:at + FRAME, b * LANES:(b + 1) * LANES] = both[
                        b * FRAME:(b + 1) * FRAME, half * LANES:(half + 1) * LANES
                    ]

    def rows(q, smooth_ref):
        done = jnp.dot(row_band_ref[q], smooth_ref[...], preferred_element_type=F32)
        for r in range(ROWS):
            at = pl.multiple_of(r * PAD + q * OCT, OCT)
            for b in range(VISITS):
                wide_ref[b, pl.ds(at, OCT), :] = done[
                    r * OCT:(r + 1) * OCT, b * LANES:(b + 1) * LANES
                ]

    def two(i, carry):
        columns(2 * i + 1, odd_ref)
        rows(2 * i, even_ref)
        columns(2 * i + 2, even_ref)
        rows(2 * i + 1, odd_ref)
        return carry

    columns(0, even_ref)
    lax.fori_loop(0, OCTS // 2 - 1, two, 0)
    columns(OCTS - 1, odd_ref)
    rows(OCTS - 2, even_ref)
    rows(OCTS - 1, odd_ref)

    def gram_step(g, total):
        pieces = []
        for i in range(SPAN):
            at = pl.multiple_of((g * SPAN + i) * PAD, PAD)
            for b in range(VISITS):
                piece = wide_ref[b, pl.ds(at, PAD), :].astype(BF16)
                basis_ref[b, pl.ds(at, PAD), :] = piece
                pieces.append(piece)
        images = jnp.concatenate(pieces, axis=1)
        return total + lax.dot_general(
            images, images, (((1,), (1,)), ((), ())), preferred_element_type=F32
        )

    gram = lax.fori_loop(0, ROWS // SPAN, gram_step, jnp.zeros((PAD, PAD), F32))
    gram = jnp.concatenate([gram, jnp.zeros((PAD, LANES - PAD), F32)], axis=1)
    lane = iota((TILE, LANES), 1)
    part = gram[:TILE]
    part = jnp.where(lane >= TILE, pltpu.roll(gram[TILE:2 * TILE], TILE, 1), part)
    rest = jnp.where(lane >= 3 * TILE, pltpu.roll(gram[2 * TILE:], 3 * TILE, 1), part)
    for i in range(3):
        piece = rest.astype(BF16)
        basis_ref[0, ROWS * PAD + i * TILE:ROWS * PAD + (i + 1) * TILE, :] = piece
        rest = rest - piece.astype(F32)


def moment_kernel(
    got_ref, basis_ref, science_hbm, part_ref, science_ref, sem
):
    gots = []
    for slot in range(2):
        got = got_ref[:, slot * SUB:(slot + 1) * SUB, :].astype(F32)
        gots.append(got.reshape(STRIPS // 2, 2 * COLS).astype(BF16))
    science = jnp.zeros((ROWS, COLS), F32)
    for slot in range(2):
        got = gots[slot]
        for half in range(2):
            science = science + lax.dot_general(
                basis_ref[1 + slot * 2 + half, ROWS * PAD:ROWS * PAD + STRIPS // 2, :ROWS],
                got[:, half * COLS:(half + 1) * COLS],
                (((0,), (0,)), ((), ())),
                preferred_element_type=F32,
            )
    science_ref[...] = science
    keep = pltpu.make_async_copy(science_ref, science_hbm, sem)
    keep.start()

    def step(g, total):
        lines = science_ref[pl.ds(pl.multiple_of(g * SUB, SUB), SUB), :]
        for b in range(VISITS):
            for i in range(SUB):
                at = pl.multiple_of((g * SUB + i) * PAD, PAD)
                total = total + basis_ref[b, pl.ds(at, PAD), :].astype(F32) * lines[i:i + 1, b * LANES:(b + 1) * LANES]
        return total

    total = lax.fori_loop(0, ROWS // SUB, step, jnp.zeros((PAD, LANES), F32))
    moment = jnp.sum(total, axis=1, keepdims=True)
    lane = iota((TILE, LANES), 1)
    part = jnp.zeros((TILE, LANES), F32)
    for i in (2, 1, 0):
        at = ROWS * PAD + i * TILE
        part = part + basis_ref[0, at:at + TILE, :].astype(F32)
    for i in range(3):
        part = jnp.where(lane == 6 * TILE + i, moment[i * TILE:(i + 1) * TILE], part)
    for v in range(part_ref.shape[0]):
        part_ref[v] = part
    keep.wait()


def solve_kernel(science_hbm, parts_ref, basis_ref, diff_ref, coeff_ref, science_ref, sems):
    copies = fetch([(science_hbm, science_ref)], sems)
    part = parts_ref[0]
    for i in range(1, parts_ref.shape[0]):
        part = part + parts_ref[i]
    lane = iota((PAD, LANES), 1)
    sub = iota((PAD, LANES), 0)
    lower = jnp.concatenate(
        [part, pltpu.roll(part, LANES - TILE, 1), pltpu.roll(part, LANES - 3 * TILE, 1)], axis=0
    )
    lower = jnp.where(lane // TILE <= sub // TILE, lower, 0.0)
    square = jnp.concatenate([lower, jnp.zeros((LANES - PAD, LANES), F32)], axis=0)
    system = jnp.where(lane // TILE > sub // TILE, square.T[:PAD], lower)
    moment = jnp.concatenate(
        [part[:, 6 * TILE + i:6 * TILE + i + 1] for i in range(3)], axis=0
    )
    system = jnp.where(lane == NB, moment, system)
    ahead = [jnp.broadcast_to(system[:, p:p + 1], (PAD, LANES)) for p in range(AHEAD)]
    for p in range(NB):
        column = ahead.pop(0)
        inverse = 1.0 / column[p:p + 1, :]
        here = sub == p

        def step(values):
            row = values[p:p + 1, :] * inverse
            return jnp.where(here, row, values - column * row)

        ahead = [step(values) for values in ahead]
        system = step(system)
        later = p + AHEAD
        if later <= NB:
            ahead.append(jnp.broadcast_to(system[:, later:later + 1], (PAD, LANES)))
    answer = ahead[0]
    coeff_ref[...] = jnp.sum(jnp.where(sub == lane, answer, 0.0), axis=0, keepdims=True)
    row = iota((SUB, LANES), 0)
    copies[0].wait()

    def step(g, carry):
        here = pl.ds(pl.multiple_of(g * SUB, SUB), SUB)
        for b in range(VISITS):
            sums = []
            for i in range(SUB):
                at = pl.multiple_of((g * SUB + i) * PAD, PAD)
                product = basis_ref[b, pl.ds(at, PAD), :].astype(F32) * answer
                total = product[:SUB]
                for n in range(1, PAD // SUB):
                    total = total + product[n * SUB:(n + 1) * SUB]
                sums.append(total)
            span = SUB // 2
            while span:
                keep = (row // span) % 2 == 0
                sums = [
                    jnp.where(keep, sums[i], sums[i + span])
                    + pltpu.roll(jnp.where(keep, sums[i + span], sums[i]), span, 0)
                    for i in range(span)
                ] if span == SUB // 2 else merge(sums, keep, span)
                span //= 2
            cut = slice(b * LANES, (b + 1) * LANES)
            diff_ref[here, cut] = science_ref[here, cut] - sums[0]
        return carry

    lax.fori_loop(0, ROWS // SUB, step, 0)


def merge(sums, keep, span):
    half = len(sums) // 2
    out = []
    for i in range(half):
        a, b = sums[i], sums[i + half]
        low = jnp.where(keep, a, b)
        high = jnp.where(keep, b, a)
        moved = jnp.where(keep, pltpu.roll(high, SUB - span, 0), pltpu.roll(high, span, 0))
        out.append(low + moved)
    return out


def share(block, axis):
    return lax.all_to_all(block, axis, 0, 0, tiled=True)


def body(template, science_src, target_rows, row_taps, col_taps):
    inner = [(i, i ^ 1) for i in range(STRIPS)]
    outer = [(i, i + 1 if i % 2 else i - 1) for i in range(1, STRIPS - 1)]
    copied = jnp.broadcast_to(template[None], (VISITS, ROWS, LANES))
    tiles = share(copied, "visit")
    targets = target_rows.reshape(STRIPS // 2, 2 * SRC)
    (outgoing,) = call(
        prepare_kernel,
        [((STRIPS, TILE, LANES), BF16)],
        targets,
        science_src[0],
        scratch=[
            pltpu.VMEM(targets.shape, jnp.int32),
            pltpu.VMEM((SRC, COLS), BF16),
            pltpu.SemaphoreType.DMA((2,)),
        ],
        far=2,
    )
    incoming = share(outgoing, STRIP)
    far_tiles = lax.ppermute(tiles, STRIP, outer)
    near_tiles = lax.ppermute(tiles, STRIP, inner)
    row_bands, col_bands, hit, own = call(
        bands_kernel,
        [((OCTS, OCT * ROWS, OCT * FRAME), BF16), ((PAD // 2, 2 * LANES, 2 * LANES), BF16), ((4, STRIPS // 2, LANES), BF16), (tiles.shape, BF16)],
        row_taps.T,
        col_taps.T,
        targets,
        tiles,
        scratch=[
            pltpu.VMEM((TAPS, NB), BF16),
            pltpu.VMEM((TAPS, NB), BF16),
            pltpu.VMEM(targets.shape, jnp.int32),
            pltpu.VMEM((LANES, LANES), F32),
            pltpu.SemaphoreType.DMA((4,)),
        ],
        far=4,
    )
    (basis,) = call(
        basis_kernel,
        [((VISITS, ROWS * PAD + 3 * TILE, LANES), BF16)],
        own,
        far_tiles,
        near_tiles,
        row_bands,
        col_bands,
        hit,
        scratch=[
            pltpu.VMEM((VISITS * FRAME, 2 * LANES), BF16),
            pltpu.VMEM((OCT * FRAME, COLS), BF16),
            pltpu.VMEM((OCT * FRAME, COLS), BF16),
            pltpu.VMEM((VISITS, ROWS * PAD, LANES), F32),
        ],
        grant=24,
    )
    science, part = call(
        moment_kernel,
        [((ROWS, COLS), F32), ((VISITS, TILE, LANES), F32)],
        incoming,
        basis,
        scratch=[pltpu.VMEM((ROWS, COLS), F32), pltpu.SemaphoreType.DMA],
        stay=1,
    )
    near = jnp.sum(share(part, ("x", "core")), axis=0)
    parts = share(jnp.broadcast_to(near[None], (VISITS, TILE, LANES)), "y")
    difference, coeffs = call(
        solve_kernel,
        [((ROWS, COLS), F32), ((1, LANES), F32)],
        science,
        parts,
        basis,
        scratch=[pltpu.VMEM((ROWS, COLS), F32), pltpu.SemaphoreType.DMA((1,))],
        far=1,
    )
    return difference[None], coeffs[:, :NB]


def solution(mesh):
    sizes = (VISITS, 8, 4, 2)
    fine = Mesh(mesh.devices.reshape(sizes), ("visit",) + STRIP)
    in_specs = (P(STRIP, "visit"), P("visit", STRIP, None), P("visit", None), P(), P())
    out_specs = (P("visit", STRIP, None), P("visit", None))
    return jax.shard_map(body, mesh=fine, in_specs=in_specs, out_specs=out_specs, check_vma=False)
```
